32 devices in a mesh: inp: 16 (over z, y, core), tm: 2 (over x).
Axes of the slice: x: 2, y: 2, z: 4, core: 2. Of those that a mesh axis runs over, the one named last changes fastest.
Arguments:
- voltages: bfloat16 [1024, 12288], P('inp', 'tm'), may hold values from -6 to 6
- tap_weights: float32 [4, 2048], replicated, may hold values from -3 to 3
- pair_offsets: int32 [4], replicated, may hold values from 1 to 15, as said below
Outputs:
- cross_vis: bfloat16 [4, 1024, 1024, 128], P(None, 'tm', 'inp')
- auto_vis: bfloat16 [1024, 1024, 128], P('tm', 'inp')
The draws below stay inside these ranges and needn't reach their ends.
Inputs may be any that keep to these rules, and one draw needn't show every extreme that they name: `pair_offsets`: the offsets are distinct.
All inputs are finite; a program needn't handle non-finite values.
Results may differ from the reference program's by a relative error of at most 0.0082.
Values may be sent and summed in bfloat16 or wider, within the bound.
No kernel may reach another device: no remote copies, remote signals or barrier semaphores. Data moves between devices by JAX's collectives and lax.ppermute only.
A program may use at most 128 MiB of HBM per device.

```python
import math
import jax
import jax.numpy as jnp
from jax import lax

NCH = 1024
INP_DEV = 64
TAPS = 4
ROUNDS = 4
FRAME = 2048
INPUTS = 1024
SPECTRA = 6
SAMPLES = 12288
N_INP = 16


def draw_pair_offsets(key, part):
    key_mid = jax.random.fold_in(key, 11)
    key_order = jax.random.fold_in(key, 23)
    middle = 2 + jax.random.permutation(key_mid, N_INP - 3)[:ROUNDS - 2]
    values = jnp.concatenate([jnp.array([1, N_INP - 1], dtype=jnp.int32), middle.astype(jnp.int32)])
    shuffle = jax.random.permutation(key_order, ROUNDS)
    return values[shuffle]


def block_levels(stream_key, dims, cuts, low, top_value):
    gain, own = 1.0, jax.random.fold_in(stream_key, 6)
    for dim, parts in cuts:
        draws = jnp.exp(jax.random.uniform(jax.random.fold_in(own, dim), (parts,), jnp.float32, low / len(cuts), top_value / len(cuts)))
        gain = gain * jnp.repeat(draws, dims[dim] // parts).reshape([-1 if axis == dim else 1 for axis in range(len(dims))])
    return gain


def scatter_about(rng, shape, deviation, limit, cuts=(), kind=jnp.bfloat16):
    entries = deviation * jax.random.normal(rng, shape, jnp.float32)
    if cuts:
        entries = entries * block_levels(rng, shape, cuts, -0.22, 0.18)
    return jnp.clip(entries, -limit, limit).astype(kind)


def setup_inputs(seed: int = 0) -> dict:
    seeds = jax.random.split(jax.random.key(seed), 4)
    voltages = scatter_about(seeds[0], (INPUTS, SAMPLES), 1.0, 6.0, ((0, 16), (1, 2)))
    tap_weights = scatter_about(seeds[1], (TAPS, FRAME), 0.5, 3.0, (), jnp.float32)
    pair_offsets = draw_pair_offsets(jax.random.fold_in(seeds[3], 71), 0)
    return dict(voltages=voltages, tap_weights=tap_weights, pair_offsets=pair_offsets)


def dft_table(frame_len):
    chan_count = frame_len // 2
    sample_idx = jnp.arange(frame_len, dtype=jnp.int32)[:, None]
    chan_idx = jnp.arange(chan_count, dtype=jnp.int32)[None, :]
    phase_arg = (sample_idx * chan_idx % frame_len).astype(jnp.float32) * (2.0 * math.pi / frame_len)
    scale_factor = 1.0 / math.sqrt(frame_len)
    return (jnp.concatenate([jnp.cos(phase_arg), -jnp.sin(phase_arg)], axis=1) * scale_factor).astype(jnp.bfloat16)

def filter_frames(extended, tap_weights, spec_count):
    tap_count = tap_weights.shape[0]
    summed = extended[:, 0:spec_count, :].astype(jnp.float32) * tap_weights[0]
    for tap_idx in range(1, tap_count):
        summed = summed + extended[:, tap_idx:tap_idx + spec_count, :].astype(jnp.float32) * tap_weights[tap_idx]
    return summed.astype(jnp.bfloat16)

def visibility(own_rows, theirs, spec_total):
    half_width = own_rows.shape[2] // 2
    products = jnp.einsum('ksi,ksj->kij', own_rows.astype(jnp.float32), theirs.astype(jnp.float32))
    real_part = products[:, :half_width, :half_width] + products[:, half_width:, half_width:]
    imag_part = products[:, half_width:, :half_width] - products[:, :half_width, half_width:]
    return (jnp.concatenate([real_part, imag_part], axis=2) / spec_total).astype(jnp.bfloat16)

def reference(voltages, tap_weights, pair_offsets):
    history = (TAPS - 1) * FRAME
    padded = jnp.concatenate([jnp.zeros((INPUTS, history), voltages.dtype), voltages], axis=1)
    padded = padded.reshape(INPUTS, SPECTRA + TAPS - 1, FRAME)
    frames = filter_frames(padded, tap_weights, SPECTRA)
    table = dft_table(FRAME)
    spectra = jnp.dot(frames.reshape(INPUTS * SPECTRA, FRAME), table, preferred_element_type=jnp.float32).astype(jnp.bfloat16)
    blocks = spectra.reshape(N_INP, INP_DEV, SPECTRA, 2, NCH).transpose(0, 4, 2, 3, 1).reshape(N_INP, NCH, SPECTRA, 2 * INP_DEV)
    auto_blocks = lax.map(lambda block_data: visibility(block_data, block_data, SPECTRA), blocks)
    auto_vis = auto_blocks.transpose(1, 0, 2, 3).reshape(NCH, INPUTS, 2 * INP_DEV)
    block_ids = jnp.arange(N_INP, dtype=jnp.int32)

    def one_round(offset_value):
        partners = ((block_ids + offset_value) % N_INP).astype(jnp.int32)
        paired = lax.map(lambda pair_args: visibility(pair_args[0], blocks[pair_args[1]], SPECTRA), (blocks, partners))
        return paired.transpose(1, 0, 2, 3).reshape(NCH, INPUTS, 2 * INP_DEV)
    cross_vis = lax.map(one_round, pair_offsets)
    return (cross_vis, auto_vis)
```

```python
import functools
import math

import jax
import jax.numpy as jnp
from jax import lax
from jax.experimental import pallas as pl
from jax.experimental.pallas import tpu as pltpu
from jax.sharding import PartitionSpec as P

GROUP = 16
HALF = GROUP // 2
VMEM_BYTES = 48 << 20


def from_ahead(block, distance):
    count = lax.axis_size("inp")
    return lax.ppermute(
        block, "inp", [(i, (i - distance) % count) for i in range(count)]
    )


def dft_table(frame_len, chan_dev):
    fine = 64
    columns = jnp.arange(2 * chan_dev, dtype=jnp.int32)
    chan_idx = (
        lax.axis_index("tm") * chan_dev
        + columns // (2 * GROUP) * GROUP
        + columns % GROUP
    )
    quarter = columns // GROUP % 2 * (frame_len // 4)
    turn = 2.0 * math.pi / frame_len
    coarse_idx = jnp.arange(frame_len // fine, dtype=jnp.int32)[:, None] * fine
    fine_idx = jnp.arange(fine, dtype=jnp.int32)[:, None]
    coarse = (coarse_idx * chan_idx % frame_len).astype(jnp.float32) * turn
    rest = ((fine_idx * chan_idx + quarter) % frame_len).astype(jnp.float32) * turn
    scale = 1.0 / math.sqrt(frame_len)
    parts = (jnp.cos(coarse) * scale, jnp.sin(coarse) * scale, jnp.cos(rest), jnp.sin(rest))
    cos_a, sin_a, cos_b, sin_b = lax.optimization_barrier(parts)
    table = cos_a[:, None] * cos_b[None] - sin_a[:, None] * sin_b[None]
    return table.astype(jnp.bfloat16).reshape(frame_len, 2 * chan_dev)


def spectra_kernel(own_at, *refs):
    *volt_refs, taps_ref, table_ref, out_ref, frames = refs
    rows, samples_dev = volt_refs[0].shape[-2:]
    tap_count, frame_len = taps_ref.shape
    spec_dev = samples_dev // frame_len
    spec_total = frames.shape[0] // rows
    width = 2 * GROUP * spec_total

    @pl.when(pl.program_id(0) == 0)
    def _():
        def frame(index, cols):
            part = index // spec_dev
            at = pl.ds(index % spec_dev * frame_len + cols, chunk)
            if len(volt_refs) == 2:
                here = own_at[0] == part
                return jnp.where(here, volt_refs[0][:, at], volt_refs[1][:, at]).astype(jnp.float32)
            return volt_refs[0][part, :, at].astype(jnp.float32)

        chunk = 256
        for cols in range(0, frame_len, chunk):
            pieces = [frame(index, cols) for index in range(spec_total)]
            for spec in range(spec_total):
                total = None
                for tap in range(tap_count):
                    index = spec + tap - (tap_count - 1)
                    if index >= 0:
                        term = pieces[index] * taps_ref[tap : tap + 1, cols : cols + chunk]
                        total = term if total is None else total + term
                frames[spec * rows : (spec + 1) * rows, cols : cols + chunk] = total.astype(
                    jnp.bfloat16
                )

    spectra = jnp.dot(frames[...], table_ref[...], preferred_element_type=jnp.float32)
    for group in range(table_ref.shape[1] // (2 * GROUP)):
        lanes = slice(group * 2 * GROUP, (group + 1) * 2 * GROUP)
        packed = jnp.concatenate(
            [spectra[s * rows : (s + 1) * rows, lanes] for s in range(spec_total)], axis=1
        )
        out_ref[:, group * width : (group + 1) * width] = packed.astype(jnp.bfloat16)


def block_spectra(own_at, volts, tap_weights, table, spec_total):
    rows = volts[0].shape[-2]
    frame_len, cols = table.shape
    step = min(cols, 256)
    width = cols * spec_total
    steps = cols // step

    def whole(array):
        return pl.BlockSpec(array.shape, lambda i, at: (0,) * array.ndim)

    return pl.pallas_call(
        spectra_kernel,
        grid_spec=pltpu.PrefetchScalarGridSpec(
            num_scalar_prefetch=1,
            grid=(steps,),
            in_specs=[whole(v) for v in volts]
            + [whole(tap_weights), pl.BlockSpec((frame_len, step), lambda i, at: (0, i))],
            out_specs=pl.BlockSpec((rows, width // steps), lambda i, at: (0, i)),
            scratch_shapes=[pltpu.VMEM((spec_total * rows, frame_len), jnp.bfloat16)],
        ),
        out_shape=jax.ShapeDtypeStruct((rows, width), jnp.bfloat16),
        compiler_params=pltpu.CompilerParams(vmem_limit_bytes=VMEM_BYTES),
        cost_estimate=pl.CostEstimate(
            flops=2 * rows * spec_total * frame_len * cols,
            bytes_accessed=2 * (frame_len * cols + 2 * rows * width),
            transcendentals=0,
        ),
        name="spectra",
    )(own_at, *volts, tap_weights, table)


def vis_kernel(spec_total, own_ref, their_ref, *refs):
    out_ref = refs[-1]
    rows, block = own_ref.shape
    width = 2 * GROUP * spec_total
    for group in range(block // width):
        first = group * width
        low = first // 128 * 128
        high = -(-(first + width) // 128) * 128
        lane = lax.broadcasted_iota(jnp.int32, (rows, high - low), 1) + (low - first)
        inside = (lane >= 0) & (lane < width)
        chan = lane % GROUP
        mine = own_ref[:, low:high]
        theirs = their_ref[:, low:high].astype(jnp.float32)
        span = high - low
        turned = jnp.where(
            lane // GROUP % 2 == 0,
            -pltpu.roll(theirs, span - GROUP, 1),
            pltpu.roll(theirs, GROUP, 1),
        )
        zero = jnp.zeros_like(theirs)
        lower, upper = inside & (chan < HALF), inside & (chan >= HALF)
        right = jnp.concatenate(
            [
                jnp.where(lower, theirs, zero),
                jnp.where(lower, turned, zero),
                jnp.where(upper, theirs, zero),
                jnp.where(upper, turned, zero),
            ],
            axis=0,
        ).astype(jnp.bfloat16)
        left = jnp.concatenate(
            [
                jnp.where(inside & (chan % HALF == c), mine, jnp.zeros_like(mine))
                for c in range(HALF)
            ],
            axis=0,
        )
        product = lax.dot_general(
            left, right, (((1,), (1,)), ((), ())), preferred_element_type=jnp.float32
        ) * (1.0 / spec_total)
        product = product.astype(jnp.bfloat16)
        for c in range(HALF):
            at = group * GROUP + c
            piece = product[c * rows : (c + 1) * rows]
            out_ref[at] = piece[:, : 2 * rows]
            out_ref[at + HALF] = piece[:, 2 * rows :]


def visibility(own, theirs, spec_total, chan_dev, slot=None, rounds=None, into=None):
    rows, lanes = own.shape
    width = 2 * GROUP * spec_total
    groups = math.gcd(chan_dev // GROUP, 4)
    shape = (chan_dev, rows, 2 * rows)
    block = (groups * GROUP, rows, 2 * rows)
    if rounds is None:
        out_spec = pl.BlockSpec(block, lambda i: (i, 0, 0))
    else:
        shape = (rounds,) + shape
        out_spec = pl.BlockSpec((None,) + block, lambda i: (slot, i, 0, 0))
    spec = pl.BlockSpec((rows, groups * width), lambda i: (0, i))
    args, specs, alias = [own, theirs], [spec, spec], {}
    if into is not None:
        args.append(into)
        specs.append(pl.BlockSpec(memory_space=pl.ANY))
        alias = {2: 0}
    return pl.pallas_call(
        functools.partial(vis_kernel, spec_total),
        grid=(chan_dev // (groups * GROUP),),
        in_specs=specs,
        out_specs=out_spec,
        out_shape=jax.ShapeDtypeStruct(shape, jnp.bfloat16),
        input_output_aliases=alias,
        compiler_params=pltpu.CompilerParams(vmem_limit_bytes=VMEM_BYTES),
        cost_estimate=pl.CostEstimate(
            flops=2 * chan_dev * rows * 2 * rows * 2 * GROUP * spec_total,
            bytes_accessed=2 * (2 * rows * lanes + chan_dev * rows * 2 * rows),
            transcendentals=0,
        ),
        name="vis",
    )(*args)


def per_device(voltages, tap_weights, pair_offsets):
    rows, samples_dev = voltages.shape
    frame_len = tap_weights.shape[1]
    tm_count = lax.axis_size("tm")
    block_total = lax.axis_size("inp")
    chan_dev = frame_len // 2 // tm_count
    spec_total = samples_dev * tm_count // frame_len
    round_count = pair_offsets.shape[0]

    own_at = lax.axis_index("tm").astype(jnp.int32).reshape(1)
    if tm_count == 2:
        volts = [voltages, lax.ppermute(voltages, "tm", [(0, 1), (1, 0)])]
    else:
        volts = [lax.all_gather(voltages, "tm")]
    table = dft_table(frame_len, chan_dev)
    own = block_spectra(own_at, volts, tap_weights, table, spec_total)

    branches = [
        functools.partial(from_ahead, distance=distance) for distance in range(1, block_total)
    ]
    auto = visibility(own, own, spec_total, chan_dev)
    cross = None
    for slot in range(round_count):
        theirs = lax.switch(pair_offsets[slot] - 1, branches, own)
        cross = visibility(own, theirs, spec_total, chan_dev, slot, round_count, cross)
    return cross, auto


def solution(mesh):
    in_specs = (P("inp", "tm"), P(), P())
    out_specs = (P(None, "tm", "inp", None), P("tm", "inp", None))
    return jax.shard_map(
        per_device, mesh=mesh, in_specs=in_specs, out_specs=out_specs, check_vma=False
    )
```

```python
import functools
import math

import jax
import jax.numpy as jnp
from jax import lax
from jax.experimental import pallas as pl
from jax.experimental.pallas import tpu as pltpu
from jax.sharding import PartitionSpec as P

GROUP = 16
HALF = GROUP // 2
VMEM_BYTES = 48 << 20
VIS_BYTES = 12 << 20


def from_ahead(block, distance):
    count = lax.axis_size("inp")
    return lax.ppermute(
        block, "inp", [(i, (i - distance) % count) for i in range(count)]
    )


def circle(steps, count):
    quarter = (steps + count // 8) // (count // 4)
    x = (steps - quarter * (count // 4)).astype(jnp.float32) * (2.0 * math.pi / count)
    square = x * x
    even = jnp.float32(-1.0 / math.factorial(10))
    odd = jnp.float32(1.0 / math.factorial(9))
    for power in (8, 6, 4, 2, 0):
        even = even * square + (-1.0) ** (power // 2) / math.factorial(power)
    for power in (7, 5, 3, 1):
        odd = odd * square + (-1.0) ** (power // 2) / math.factorial(power)
    odd = odd * x
    cross = quarter % 2 == 1
    cosine = jnp.where(cross, odd, even)
    sine = jnp.where(cross, even, odd)
    quarter = quarter % 4
    cosine = jnp.where((quarter == 1) | (quarter == 2), -cosine, cosine)
    sine = jnp.where(quarter >= 2, -sine, sine)
    return cosine, sine


def table_kernel(fine, chan_dev, own_at, out_ref, cos_a, sin_a):
    frame_len, lanes = out_ref.shape
    scale = 1.0 / math.sqrt(frame_len)

    def turns(rows, stride):
        shape = (rows, lanes)
        row = lax.broadcasted_iota(jnp.int32, shape, 0) * stride
        column = lax.broadcasted_iota(jnp.int32, shape, 1) + pl.program_id(0) * lanes
        first = own_at[0] * chan_dev
        chan = first + column // (2 * GROUP) * GROUP + column % GROUP
        return row * chan, column // GROUP % 2 * (frame_len // 4)

    angle, _ = turns(frame_len // fine, fine)
    cosine, sine = circle(angle % frame_len, frame_len)
    cos_a[...] = cosine * scale
    sin_a[...] = sine * scale
    angle, quarter = turns(fine, 1)
    cos_b, sin_b = circle((angle + quarter) % frame_len, frame_len)

    def body(row, carry):
        at = pl.ds(row, 1)
        block = cos_a[at, :] * cos_b - sin_a[at, :] * sin_b
        out_ref[pl.ds(pl.multiple_of(row * fine, fine), fine), :] = block.astype(jnp.bfloat16)
        return carry

    lax.fori_loop(0, frame_len // fine, body, 0)


def dft_table(own_at, frame_len, chan_dev):
    fine, lanes = 64, 128
    part = pltpu.VMEM((frame_len // fine, lanes), jnp.float32)
    return pl.pallas_call(
        functools.partial(table_kernel, fine, chan_dev),
        grid=(2 * chan_dev // lanes,),
        in_specs=[pl.BlockSpec(memory_space=pltpu.SMEM)],
        out_specs=pl.BlockSpec((frame_len, lanes), lambda i: (0, i)),
        out_shape=pltpu.HBM((frame_len, 2 * chan_dev), jnp.bfloat16),
        scratch_shapes=[part, part],
        compiler_params=pltpu.CompilerParams(vmem_limit_bytes=VIS_BYTES),
        cost_estimate=pl.CostEstimate(
            flops=6 * frame_len * chan_dev,
            bytes_accessed=4 * frame_len * chan_dev,
            transcendentals=0,
        ),
        name="table",
    )(own_at)


def spectra_kernel(own_at, *refs):
    *volt_refs, taps_ref, table_ref, out_ref, frames = refs
    rows, samples_dev = volt_refs[0].shape[-2:]
    tap_count, frame_len = taps_ref.shape
    spec_dev = samples_dev // frame_len
    spec_total = frames.shape[0] // rows
    width = 2 * GROUP * spec_total

    @pl.when(pl.program_id(0) == 0)
    def _():
        def frame(index, cols):
            part = index // spec_dev
            at = pl.ds(index % spec_dev * frame_len + cols, chunk)
            if len(volt_refs) == 2:
                here = own_at[0] == part
                return jnp.where(here, volt_refs[0][:, at], volt_refs[1][:, at]).astype(jnp.float32)
            return volt_refs[0][part, :, at].astype(jnp.float32)

        chunk = 256
        for cols in range(0, frame_len, chunk):
            pieces = [frame(index, cols) for index in range(spec_total)]
            for spec in range(spec_total):
                total = None
                for tap in range(tap_count):
                    index = spec + tap - (tap_count - 1)
                    if index >= 0:
                        term = pieces[index] * taps_ref[tap : tap + 1, cols : cols + chunk]
                        total = term if total is None else total + term
                frames[spec * rows : (spec + 1) * rows, cols : cols + chunk] = total.astype(
                    jnp.bfloat16
                )

    spectra = jnp.dot(frames[...], table_ref[...], preferred_element_type=jnp.float32)
    for group in range(table_ref.shape[1] // (2 * GROUP)):
        lanes = slice(group * 2 * GROUP, (group + 1) * 2 * GROUP)
        packed = jnp.concatenate(
            [spectra[s * rows : (s + 1) * rows, lanes] for s in range(spec_total)], axis=1
        )
        out_ref[:, group * width : (group + 1) * width] = packed.astype(jnp.bfloat16)


def block_spectra(own_at, volts, tap_weights, table, spec_total):
    rows = volts[0].shape[-2]
    frame_len, cols = table.shape
    step = min(cols, 256)
    width = cols * spec_total
    steps = cols // step

    def whole(array):
        return pl.BlockSpec(array.shape, lambda i, at: (0,) * array.ndim)

    return pl.pallas_call(
        spectra_kernel,
        grid_spec=pltpu.PrefetchScalarGridSpec(
            num_scalar_prefetch=1,
            grid=(steps,),
            in_specs=[whole(v) for v in volts]
            + [whole(tap_weights), pl.BlockSpec((frame_len, step), lambda i, at: (0, i))],
            out_specs=pl.BlockSpec((rows, width // steps), lambda i, at: (0, i)),
            scratch_shapes=[pltpu.VMEM((spec_total * rows, frame_len), jnp.bfloat16)],
        ),
        out_shape=jax.ShapeDtypeStruct((rows, width), jnp.bfloat16),
        compiler_params=pltpu.CompilerParams(vmem_limit_bytes=VMEM_BYTES),
        cost_estimate=pl.CostEstimate(
            flops=2 * rows * spec_total * frame_len * cols,
            bytes_accessed=2 * (frame_len * cols + 2 * rows * width),
            transcendentals=0,
        ),
        name="spectra",
    )(own_at, *volts, tap_weights, table)


def vis_kernel(spec_total, jobs, unroll, base, chained, *refs):
    refs = list(refs)
    slots = None if base is None else refs.pop(0)
    own_ref, *their_refs = refs[: 1 + jobs]
    refs = refs[1 + jobs + chained :]
    out_ref, masks, buffers, sems = refs
    rows, lanes = own_ref.shape
    width = 2 * GROUP * spec_total
    groups = masks.shape[0]
    depth = buffers.shape[1]
    window = groups * width
    spans = []
    for group in range(groups):
        low = group * width // 128 * 128
        high = -(-(group + 1) * width // 128) * 128
        spans.append((low, high))
        lane = lax.broadcasted_iota(jnp.int32, (16, high - low), 1) + (low - group * width)
        inside = (lane >= 0) & (lane < width)
        chan, real = lane % GROUP, lane // GROUP % 2 == 0

        def put(index, where, value):
            masks[group, index] = jnp.where(inside & where, value, 0.0).astype(jnp.bfloat16)

        for c in range(HALF):
            put(c, chan % HALF == c, 1.0)
        for side, half in enumerate((chan < HALF, chan >= HALF)):
            put(HALF + 3 * side, half, 1.0)
            put(HALF + 3 * side + 1, half & real, -1.0)
            put(HALF + 3 * side + 2, half & ~real, 1.0)

    def copy_out(job, turn, slot):
        to = out_ref if slots is None else out_ref.at[slots[base + job]]
        count = groups * GROUP
        return pltpu.make_async_copy(
            buffers.at[job, slot], to.at[pl.ds(turn * count, count)], sems.at[job, slot]
        )

    turns = lanes // window
    unroll = math.gcd(unroll, turns)

    def body(step, carry):
        for ahead in range(unroll):
            turn = step * unroll + ahead
            for job in range(jobs):

                @pl.when(turn >= depth)
                def _():
                    copy_out(job, turn - depth, turn % depth).wait()

        for ahead in range(unroll):
            turn = step * unroll + ahead
            for group in range(groups):
                multiply(turn, group)
        for ahead in range(unroll):
            turn = step * unroll + ahead
            for job in range(jobs):
                copy_out(job, turn, turn % depth).start()
        return carry

    def multiply(turn, group):
        slot = turn % depth
        low, high = spans[group]
        span = high - low
        at = pl.ds(pl.multiple_of(turn * window + low, 128), span)

        def masked(block, index):
            tiles = block.reshape(rows // 16, 16, span) * masks[group, index][None]
            return tiles.reshape(rows, span)

        mine = own_ref[:, at]
        left = jnp.concatenate([masked(mine, c) for c in range(HALF)], axis=0)
        for job in range(jobs):
            theirs = their_refs[job][:, at]
            wide = theirs.astype(jnp.float32)
            ahead = pltpu.roll(wide, span - GROUP, 1).astype(jnp.bfloat16)
            behind = pltpu.roll(wide, GROUP, 1).astype(jnp.bfloat16)
            right = []
            for base in (HALF, HALF + 3):
                right.append(masked(theirs, base))
                right.append(masked(ahead, base + 1) + masked(behind, base + 2))
            product = lax.dot_general(
                left,
                jnp.concatenate(right, axis=0),
                (((1,), (1,)), ((), ())),
                preferred_element_type=jnp.float32,
            )
            product = (product * (1.0 / spec_total)).astype(jnp.bfloat16)
            for c in range(HALF):
                piece = product[c * rows : (c + 1) * rows]
                buffers[job, slot, group * GROUP + c] = piece[:, : 2 * rows]
                buffers[job, slot, group * GROUP + c + HALF] = piece[:, 2 * rows :]

    lax.fori_loop(0, turns // unroll, body, 0)
    for turn in range(max(turns - depth, 0), turns):
        for job in range(jobs):
            copy_out(job, turn, turn % depth).wait()


def visibility(own, theirs, spec_total, slots=None, base=None, into=None, unroll=1):
    rows, lanes = own.shape
    width = 2 * GROUP * spec_total
    chan_dev = lanes // (2 * spec_total)
    jobs = len(theirs)
    groups = min(math.lcm(width, 128) // width, chan_dev // GROUP)
    span = max(
        -(-(g + 1) * width // 128) * 128 - g * width // 128 * 128 for g in range(groups)
    )
    shape = (chan_dev, rows, 2 * rows)
    if slots is not None:
        shape = slots.shape + shape
    depth = max(4 if jobs == 1 else 2, 2 * unroll)
    in_vmem = pl.BlockSpec(memory_space=pltpu.VMEM)
    anywhere = pl.BlockSpec(memory_space=pltpu.HBM)
    args, specs, alias = [own, *theirs], [in_vmem] * (1 + jobs), {}
    if slots is not None:
        args.insert(0, slots)
        specs.insert(0, pl.BlockSpec(memory_space=pltpu.SMEM))
    if into is not None:
        alias = {len(args): 0}
        args.append(into)
        specs.append(anywhere)
    return pl.pallas_call(
        functools.partial(
            vis_kernel, spec_total, jobs, unroll, base, into is not None
        ),
        in_specs=specs,
        out_specs=anywhere,
        out_shape=pltpu.HBM(shape, jnp.bfloat16),
        scratch_shapes=[
            pltpu.VMEM((groups, HALF + 6, 16, span), jnp.bfloat16),
            pltpu.VMEM((jobs, depth, groups * GROUP, rows, 2 * rows), jnp.bfloat16),
            pltpu.SemaphoreType.DMA((jobs, depth)),
        ],
        input_output_aliases=alias,
        compiler_params=pltpu.CompilerParams(vmem_limit_bytes=VIS_BYTES),
        cost_estimate=pl.CostEstimate(
            flops=jobs * 4 * lanes * rows * rows * HALF,
            bytes_accessed=2 * (jobs + 1) * rows * lanes + 4 * jobs * chan_dev * rows * rows,
            transcendentals=0,
        ),
        name="vis",
    )(*args)


def order_rounds(pair_offsets, block_total):
    count = pair_offsets.shape[0]
    values = [pair_offsets[i] for i in range(count)]
    keys = [
        jnp.minimum(value, block_total - value) * count + i for i, value in enumerate(values)
    ]
    places = [sum((other < key).astype(jnp.int32) for other in keys) for key in keys]

    def pick(place, items):
        return sum(jnp.where(at == place, item, 0) for at, item in zip(places, items))

    offsets = [pick(place, values) for place in range(count)]
    rounds = jnp.stack([pick(place, range(count)) for place in range(count)])
    return rounds.astype(jnp.int32), offsets


def per_device(voltages, tap_weights, pair_offsets):
    rows, samples_dev = voltages.shape
    frame_len = tap_weights.shape[1]
    tm_count = lax.axis_size("tm")
    block_total = lax.axis_size("inp")
    chan_dev = frame_len // 2 // tm_count
    spec_total = samples_dev * tm_count // frame_len
    round_count = pair_offsets.shape[0]

    rounds, offsets = order_rounds(pair_offsets, block_total)
    own_at = lax.axis_index("tm").astype(jnp.int32).reshape(1)
    last = round_count - 1

    def exchange(place, beside=None):
        def branch(distance, block, *rest):
            theirs = from_ahead(block, distance)
            return (theirs,) if beside is None else (theirs, beside(block, *rest))

        def run(*args):
            branches = [functools.partial(branch, d) for d in range(1, block_total)]
            return lax.switch(offsets[place] - 1, branches, *args)

        return run

    def make_table(block, at):
        return dft_table(at, frame_len, chan_dev)

    def swapped(block):
        return [block, lax.ppermute(block, "tm", [(0, 1), (1, 0)])]

    def spectra_of(volts, table):
        return block_spectra(own_at, volts, tap_weights, table, spec_total)

    def auto_part(own):
        return visibility(own, [own], spec_total)

    def cross_part(own, slots, *theirs):
        return visibility(own, theirs, spec_total, slots, 0)

    if tm_count == 2 and block_total <= 16:
        volts = swapped(voltages)
        if last:
            raw, table = exchange(last - 1, make_table)(voltages, own_at)
        else:
            table = make_table(voltages, own_at)
        own = spectra_of(volts, table)
        theirs = []
        if last > 1:
            first, auto = exchange(0, auto_part)(own)
            theirs.append(first)
        else:
            auto = auto_part(own)
        theirs += [exchange(place)(own)[0] for place in range(1, last - 1)]
        if last:
            theirs.append(spectra_of(swapped(raw), table))
            final, cross = exchange(last, cross_part)(own, rounds, *theirs)
        else:
            final, cross = exchange(last)(own)[0], None
    else:
        table = make_table(voltages, own_at)
        own = spectra_of([lax.all_gather(voltages, "tm")], table)
        auto = auto_part(own)
        theirs = [exchange(place)(own)[0] for place in range(last)]
        final = exchange(last)(own)[0]
        cross = cross_part(own, rounds, *theirs) if last else None
    cross = visibility(own, [final], spec_total, rounds, last, cross, unroll=4)
    return cross, auto


def solution(mesh):
    in_specs = (P("inp", "tm"), P(), P())
    out_specs = (P(None, "tm", "inp", None), P("tm", "inp", None))
    return jax.shard_map(
        per_device, mesh=mesh, in_specs=in_specs, out_specs=out_specs, check_vma=False
    )
```

```python
import functools
import math

import jax
import jax.numpy as jnp
from jax import lax
from jax.experimental import pallas as pl
from jax.experimental.pallas import tpu as pltpu
from jax.sharding import PartitionSpec as P

GROUP = 16
HALF = GROUP // 2
VMEM_BYTES = 48 << 20
VIS_BYTES = 12 << 20


def from_ahead(block, distance):
    count = lax.axis_size("inp")
    return lax.ppermute(
        block, "inp", [(i, (i - distance) % count) for i in range(count)]
    )


def circle(steps, count):
    quarter = (steps + count // 8) // (count // 4)
    x = (steps - quarter * (count // 4)).astype(jnp.float32) * (2.0 * math.pi / count)
    square = x * x
    even = jnp.float32(-1.0 / math.factorial(10))
    odd = jnp.float32(1.0 / math.factorial(9))
    for power in (8, 6, 4, 2, 0):
        even = even * square + (-1.0) ** (power // 2) / math.factorial(power)
    for power in (7, 5, 3, 1):
        odd = odd * square + (-1.0) ** (power // 2) / math.factorial(power)
    odd = odd * x
    cross = quarter % 2 == 1
    cosine = jnp.where(cross, odd, even)
    sine = jnp.where(cross, even, odd)
    quarter = quarter % 4
    cosine = jnp.where((quarter == 1) | (quarter == 2), -cosine, cosine)
    sine = jnp.where(quarter >= 2, -sine, sine)
    return cosine, sine


def table_kernel(fine, chan_dev, own_at, out_ref, cos_a, sin_a):
    frame_len, lanes = out_ref.shape
    scale = 1.0 / math.sqrt(frame_len)

    def turns(rows, stride):
        shape = (rows, lanes)
        row = lax.broadcasted_iota(jnp.int32, shape, 0) * stride
        column = lax.broadcasted_iota(jnp.int32, shape, 1) + pl.program_id(0) * lanes
        first = own_at[0] * chan_dev
        chan = first + column // (2 * GROUP) * GROUP + column % GROUP
        return row * chan, column // GROUP % 2 * (frame_len // 4)

    angle, _ = turns(frame_len // fine, fine)
    cosine, sine = circle(angle % frame_len, frame_len)
    cos_a[...] = cosine * scale
    sin_a[...] = sine * scale
    angle, quarter = turns(fine, 1)
    cos_b, sin_b = circle((angle + quarter) % frame_len, frame_len)

    def body(row, carry):
        at = pl.ds(row, 1)
        block = cos_a[at, :] * cos_b - sin_a[at, :] * sin_b
        out_ref[pl.ds(pl.multiple_of(row * fine, fine), fine), :] = block.astype(jnp.bfloat16)
        return carry

    lax.fori_loop(0, frame_len // fine, body, 0)


def dft_table(own_at, frame_len, chan_dev):
    fine, lanes = 64, 128
    part = pltpu.VMEM((frame_len // fine, lanes), jnp.float32)
    return pl.pallas_call(
        functools.partial(table_kernel, fine, chan_dev),
        grid=(2 * chan_dev // lanes,),
        in_specs=[pl.BlockSpec(memory_space=pltpu.SMEM)],
        out_specs=pl.BlockSpec((frame_len, lanes), lambda i: (0, i)),
        out_shape=pltpu.HBM((frame_len, 2 * chan_dev), jnp.bfloat16),
        scratch_shapes=[part, part],
        compiler_params=pltpu.CompilerParams(vmem_limit_bytes=VIS_BYTES),
        cost_estimate=pl.CostEstimate(
            flops=6 * frame_len * chan_dev,
            bytes_accessed=4 * frame_len * chan_dev,
            transcendentals=0,
        ),
        name="table",
    )(own_at)


def spectra_kernel(own_at, *refs):
    *volt_refs, taps_ref, table_ref, out_ref, frames = refs
    rows, samples_dev = volt_refs[0].shape[-2:]
    tap_count, frame_len = taps_ref.shape
    spec_dev = samples_dev // frame_len
    spec_total = frames.shape[0] // rows
    width = 2 * GROUP * spec_total

    @pl.when(pl.program_id(0) == 0)
    def _():
        chunk = 256

        def frame(index, cols):
            part = index // spec_dev
            at = pl.ds(pl.multiple_of(index % spec_dev * frame_len + cols, chunk), chunk)
            if len(volt_refs) == 2:
                here = own_at[0] == part
                return jnp.where(here, volt_refs[0][:, at], volt_refs[1][:, at]).astype(jnp.float32)
            return volt_refs[0][part, :, at].astype(jnp.float32)

        def body(turn, carry):
            cols = pl.multiple_of(turn * chunk, chunk)
            at = pl.ds(cols, chunk)
            pieces = [frame(index, cols) for index in range(spec_total)]
            taps = [taps_ref[tap : tap + 1, at] for tap in range(tap_count)]
            for spec in range(spec_total):
                total = None
                for tap in range(tap_count):
                    index = spec + tap - (tap_count - 1)
                    if index >= 0:
                        term = pieces[index] * taps[tap]
                        total = term if total is None else total + term
                frames[spec * rows : (spec + 1) * rows, at] = total.astype(jnp.bfloat16)
            return carry

        lax.fori_loop(0, frame_len // chunk, body, 0)

    spectra = jnp.dot(frames[...], table_ref[...], preferred_element_type=jnp.float32)
    for group in range(table_ref.shape[1] // (2 * GROUP)):
        lanes = slice(group * 2 * GROUP, (group + 1) * 2 * GROUP)
        packed = jnp.concatenate(
            [spectra[s * rows : (s + 1) * rows, lanes] for s in range(spec_total)], axis=1
        )
        out_ref[:, group * width : (group + 1) * width] = packed.astype(jnp.bfloat16)


def block_spectra(own_at, volts, tap_weights, table, spec_total):
    rows = volts[0].shape[-2]
    frame_len, cols = table.shape
    step = min(cols, 256)
    width = cols * spec_total
    steps = cols // step

    def whole(array):
        return pl.BlockSpec(array.shape, lambda i, at: (0,) * array.ndim)

    return pl.pallas_call(
        spectra_kernel,
        grid_spec=pltpu.PrefetchScalarGridSpec(
            num_scalar_prefetch=1,
            grid=(steps,),
            in_specs=[whole(v) for v in volts]
            + [whole(tap_weights), pl.BlockSpec((frame_len, step), lambda i, at: (0, i))],
            out_specs=pl.BlockSpec((rows, width // steps), lambda i, at: (0, i)),
            scratch_shapes=[pltpu.VMEM((spec_total * rows, frame_len), jnp.bfloat16)],
        ),
        out_shape=jax.ShapeDtypeStruct((rows, width), jnp.bfloat16),
        compiler_params=pltpu.CompilerParams(vmem_limit_bytes=VMEM_BYTES),
        cost_estimate=pl.CostEstimate(
            flops=2 * rows * spec_total * frame_len * cols,
            bytes_accessed=2 * (frame_len * cols + 2 * rows * width),
            transcendentals=0,
        ),
        name="spectra",
    )(own_at, *volts, tap_weights, table)


def vis_kernel(spec_total, jobs, unroll, base, chained, *refs):
    refs = list(refs)
    slots = None if base is None else refs.pop(0)
    own_ref, *their_refs = refs[: 1 + jobs]
    refs = refs[1 + jobs + chained :]
    out_ref, masks, buffers, sems = refs
    rows, lanes = own_ref.shape
    width = 2 * GROUP * spec_total
    groups = masks.shape[0]
    depth = buffers.shape[1]
    window = groups * width
    spans = []
    for group in range(groups):
        low = group * width // 128 * 128
        high = -(-(group + 1) * width // 128) * 128
        spans.append((low, high))
        lane = lax.broadcasted_iota(jnp.int32, (16, high - low), 1) + (low - group * width)
        inside = (lane >= 0) & (lane < width)
        chan, real = lane % GROUP, lane // GROUP % 2 == 0

        def put(index, where, value):
            masks[group, index] = jnp.where(inside & where, value, 0.0).astype(jnp.bfloat16)

        for c in range(HALF):
            put(c, chan % HALF == c, 1.0)
        for side, half in enumerate((chan < HALF, chan >= HALF)):
            put(HALF + 3 * side, half, 1.0)
            put(HALF + 3 * side + 1, half & real, -1.0)
            put(HALF + 3 * side + 2, half & ~real, 1.0)

    def copy_out(job, turn, slot):
        to = out_ref if slots is None else out_ref.at[slots[base + job]]
        count = groups * GROUP
        return pltpu.make_async_copy(
            buffers.at[job, slot], to.at[pl.ds(turn * count, count)], sems.at[job, slot]
        )

    turns = lanes // window
    unroll = math.gcd(unroll, turns)

    def body(step, carry):
        for ahead in range(unroll):
            turn = step * unroll + ahead
            for job in range(jobs):

                @pl.when(turn >= depth)
                def _():
                    copy_out(job, turn - depth, turn % depth).wait()

        for ahead in range(unroll):
            turn = step * unroll + ahead
            for group in range(groups):
                multiply(turn, group)
        for ahead in range(unroll):
            turn = step * unroll + ahead
            for job in range(jobs):
                copy_out(job, turn, turn % depth).start()
        return carry

    def multiply(turn, group):
        slot = turn % depth
        low, high = spans[group]
        span = high - low
        at = pl.ds(pl.multiple_of(turn * window + low, 128), span)

        def masked(block, index):
            tiles = block.reshape(rows // 16, 16, span) * masks[group, index][None]
            return tiles.reshape(rows, span)

        mine = own_ref[:, at]
        left = jnp.concatenate([masked(mine, c) for c in range(HALF)], axis=0)
        for job in range(jobs):
            theirs = their_refs[job][:, at]
            wide = theirs.astype(jnp.float32)
            ahead = pltpu.roll(wide, span - GROUP, 1).astype(jnp.bfloat16)
            behind = pltpu.roll(wide, GROUP, 1).astype(jnp.bfloat16)
            right = []
            for base in (HALF, HALF + 3):
                right.append(masked(theirs, base))
                right.append(masked(ahead, base + 1) + masked(behind, base + 2))
            product = lax.dot_general(
                left,
                jnp.concatenate(right, axis=0),
                (((1,), (1,)), ((), ())),
                preferred_element_type=jnp.float32,
            )
            product = (product * (1.0 / spec_total)).astype(jnp.bfloat16)
            for c in range(HALF):
                piece = product[c * rows : (c + 1) * rows]
                buffers[job, slot, group * GROUP + c] = piece[:, : 2 * rows]
                buffers[job, slot, group * GROUP + c + HALF] = piece[:, 2 * rows :]

    lax.fori_loop(0, turns // unroll, body, 0)
    for turn in range(max(turns - depth, 0), turns):
        for job in range(jobs):
            copy_out(job, turn, turn % depth).wait()


def visibility(own, theirs, spec_total, slots=None, base=None, into=None, unroll=1):
    rows, lanes = own.shape
    width = 2 * GROUP * spec_total
    chan_dev = lanes // (2 * spec_total)
    jobs = len(theirs)
    groups = min(math.lcm(width, 128) // width, chan_dev // GROUP)
    span = max(
        -(-(g + 1) * width // 128) * 128 - g * width // 128 * 128 for g in range(groups)
    )
    shape = (chan_dev, rows, 2 * rows)
    if slots is not None:
        shape = slots.shape + shape
    depth = max(4 if jobs == 1 else 2, 2 * unroll)
    in_vmem = pl.BlockSpec(memory_space=pltpu.VMEM)
    anywhere = pl.BlockSpec(memory_space=pltpu.HBM)
    args, specs, alias = [own, *theirs], [in_vmem] * (1 + jobs), {}
    if slots is not None:
        args.insert(0, slots)
        specs.insert(0, pl.BlockSpec(memory_space=pltpu.SMEM))
    if into is not None:
        alias = {len(args): 0}
        args.append(into)
        specs.append(anywhere)
    return pl.pallas_call(
        functools.partial(
            vis_kernel, spec_total, jobs, unroll, base, into is not None
        ),
        in_specs=specs,
        out_specs=anywhere,
        out_shape=pltpu.HBM(shape, jnp.bfloat16),
        scratch_shapes=[
            pltpu.VMEM((groups, HALF + 6, 16, span), jnp.bfloat16),
            pltpu.VMEM((jobs, depth, groups * GROUP, rows, 2 * rows), jnp.bfloat16),
            pltpu.SemaphoreType.DMA((jobs, depth)),
        ],
        input_output_aliases=alias,
        compiler_params=pltpu.CompilerParams(vmem_limit_bytes=VIS_BYTES),
        cost_estimate=pl.CostEstimate(
            flops=jobs * 4 * lanes * rows * rows * HALF,
            bytes_accessed=2 * (jobs + 1) * rows * lanes + 4 * jobs * chan_dev * rows * rows,
            transcendentals=0,
        ),
        name="vis",
    )(*args)


def order_kernel(block_total, offsets_ref, rounds_ref, sorted_ref):
    count = offsets_ref.shape[0]
    values = [offsets_ref[i] for i in range(count)]
    keys = [
        jnp.minimum(value, block_total - value) * count + i for i, value in enumerate(values)
    ]
    for i in range(count):
        place = sum(jnp.where(key < keys[i], 1, 0) for key in keys)
        rounds_ref[place] = i
        sorted_ref[place] = values[i] - 1


def order_rounds(pair_offsets, block_total):
    like = jax.ShapeDtypeStruct(pair_offsets.shape, jnp.int32)
    in_smem = pl.BlockSpec(memory_space=pltpu.SMEM)
    return pl.pallas_call(
        functools.partial(order_kernel, block_total),
        in_specs=[in_smem],
        out_specs=[in_smem, in_smem],
        out_shape=[like, like],
        name="order",
    )(pair_offsets)


def per_device(voltages, tap_weights, pair_offsets):
    rows, samples_dev = voltages.shape
    frame_len = tap_weights.shape[1]
    tm_count = lax.axis_size("tm")
    block_total = lax.axis_size("inp")
    chan_dev = frame_len // 2 // tm_count
    spec_total = samples_dev * tm_count // frame_len
    round_count = pair_offsets.shape[0]

    rounds, offsets = order_rounds(pair_offsets, block_total)
    own_at = lax.axis_index("tm").astype(jnp.int32).reshape(1)
    last = round_count - 1

    def exchange(place, beside=None):
        def branch(distance, block, *rest):
            theirs = from_ahead(block, distance)
            return (theirs,) if beside is None else (theirs, beside(block, *rest))

        def run(*args):
            branches = [functools.partial(branch, d) for d in range(1, block_total)]
            return lax.switch(offsets[place], branches, *args)

        return run

    def make_table(block, at):
        return dft_table(at, frame_len, chan_dev)

    def swapped(block):
        return [block, lax.ppermute(block, "tm", [(0, 1), (1, 0)])]

    def spectra_of(volts, table):
        return block_spectra(own_at, volts, tap_weights, table, spec_total)

    def spectra_part(own, at, taps, table, *volts):
        return block_spectra(at, volts, taps, table, spec_total)

    def auto_part(own):
        return visibility(own, [own], spec_total)

    def cross_part(own, slots, *theirs):
        return visibility(own, theirs, spec_total, slots, 0)

    if tm_count == 2 and block_total <= 16:
        volts = swapped(voltages)
        if last:
            raw, table = exchange(last - 1, make_table)(voltages, own_at)
        else:
            table = make_table(voltages, own_at)
        own = spectra_of(volts, table)
        if last:
            raw = swapped(raw)
        theirs, hidden = [], None
        if last > 1:
            first, auto = exchange(0, auto_part)(own)
            theirs.append(first)
        else:
            auto = auto_part(own)
        for place in range(1, last - 1):
            if hidden is None:
                nearer, hidden = exchange(place, spectra_part)(
                    own, own_at, tap_weights, table, *raw
                )
            else:
                nearer = exchange(place)(own)[0]
            theirs.append(nearer)
        if last:
            theirs.append(spectra_of(raw, table) if hidden is None else hidden)
            final, cross = exchange(last, cross_part)(own, rounds, *theirs)
        else:
            final, cross = exchange(last)(own)[0], None
    else:
        table = make_table(voltages, own_at)
        own = spectra_of([lax.all_gather(voltages, "tm")], table)
        auto = auto_part(own)
        theirs = [exchange(place)(own)[0] for place in range(last)]
        final = exchange(last)(own)[0]
        cross = cross_part(own, rounds, *theirs) if last else None
    cross = visibility(own, [final], spec_total, rounds, last, cross, unroll=4)
    return cross, auto


def solution(mesh):
    in_specs = (P("inp", "tm"), P(), P())
    out_specs = (P(None, "tm", "inp", None), P("tm", "inp", None))
    return jax.shard_map(
        per_device, mesh=mesh, in_specs=in_specs, out_specs=out_specs, check_vma=False
    )
```

```python
import functools
import math

import jax
import jax.numpy as jnp
from jax import lax
from jax.experimental import pallas as pl
from jax.experimental.pallas import tpu as pltpu
from jax.sharding import PartitionSpec as P

GROUP = 16
HALF = GROUP // 2
VMEM_BYTES = 48 << 20
VIS_BYTES = 12 << 20


def from_ahead(block, distance):
    count = lax.axis_size("inp")
    return lax.ppermute(
        block, "inp", [(i, (i - distance) % count) for i in range(count)]
    )


def circle(steps, count):
    quarter = (steps + count // 8) // (count // 4)
    x = (steps - quarter * (count // 4)).astype(jnp.float32) * (2.0 * math.pi / count)
    square = x * x
    even = jnp.float32(-1.0 / math.factorial(10))
    odd = jnp.float32(1.0 / math.factorial(9))
    for power in (8, 6, 4, 2, 0):
        even = even * square + (-1.0) ** (power // 2) / math.factorial(power)
    for power in (7, 5, 3, 1):
        odd = odd * square + (-1.0) ** (power // 2) / math.factorial(power)
    odd = odd * x
    cross = quarter % 2 == 1
    cosine = jnp.where(cross, odd, even)
    sine = jnp.where(cross, even, odd)
    quarter = quarter % 4
    cosine = jnp.where((quarter == 1) | (quarter == 2), -cosine, cosine)
    sine = jnp.where(quarter >= 2, -sine, sine)
    return cosine, sine


def table_kernel(fine, chan_dev, own_at, out_ref, cos_a, sin_a, cos_b, sin_b):
    frame_len, lanes = out_ref.shape
    scale = 1.0 / math.sqrt(frame_len)
    shape = (8, lanes)
    column = lax.broadcasted_iota(jnp.int32, shape, 1) + pl.program_id(0) * lanes
    chan = own_at[0] * chan_dev + column // (2 * GROUP) * GROUP + column % GROUP
    quarter = column // GROUP % 2 * (frame_len // 4)
    row = lax.broadcasted_iota(jnp.int32, shape, 0)

    def coarse_rows(turn, carry):
        at = pl.ds(pl.multiple_of(turn * 8, 8), 8)
        cosine, sine = circle((row + turn * 8) * fine * chan % frame_len, frame_len)
        cos_a[at, :] = cosine * scale
        sin_a[at, :] = sine * scale
        return carry

    def fine_rows(turn, carry):
        at = pl.ds(pl.multiple_of(turn * 8, 8), 8)
        steps = ((row + turn * 8) * chan + quarter) % frame_len
        cos_b[at, :], sin_b[at, :] = circle(steps, frame_len)
        return carry

    def body(turn, carry):
        at = pl.ds(turn, 1)
        block = cos_a[at, :] * cos_b[...] - sin_a[at, :] * sin_b[...]
        out_ref[pl.ds(pl.multiple_of(turn * fine, fine), fine), :] = block.astype(jnp.bfloat16)
        return carry

    lax.fori_loop(0, frame_len // fine // 8, coarse_rows, 0)
    lax.fori_loop(0, fine // 8, fine_rows, 0)
    lax.fori_loop(0, frame_len // fine, body, 0)


def dft_table(own_at, frame_len, chan_dev):
    fine, lanes = 64, 128
    parts = [pltpu.VMEM((frame_len // fine, lanes), jnp.float32)] * 2
    parts += [pltpu.VMEM((fine, lanes), jnp.float32)] * 2
    return pl.pallas_call(
        functools.partial(table_kernel, fine, chan_dev),
        grid=(2 * chan_dev // lanes,),
        in_specs=[pl.BlockSpec(memory_space=pltpu.SMEM)],
        out_specs=pl.BlockSpec((frame_len, lanes), lambda i: (0, i)),
        out_shape=pltpu.HBM((frame_len, 2 * chan_dev), jnp.bfloat16),
        scratch_shapes=parts,
        compiler_params=pltpu.CompilerParams(vmem_limit_bytes=VIS_BYTES),
        cost_estimate=pl.CostEstimate(
            flops=6 * frame_len * chan_dev,
            bytes_accessed=4 * frame_len * chan_dev,
            transcendentals=0,
        ),
        name="table",
    )(own_at)


def spectra_kernel(pieces_of_sum, own_at, *refs):
    *volt_refs, taps_ref, table_ref, out_ref, frames, sums = refs
    rows, samples_dev = volt_refs[0].shape[-2:]
    tap_count, frame_len = taps_ref.shape
    spec_dev = samples_dev // frame_len
    spec_total = frames.shape[0] // rows
    width = 2 * GROUP * spec_total

    @pl.when(pl.program_id(0) == 0)
    def _():
        chunk = 256

        def frame(index, cols):
            part = index // spec_dev
            at = pl.ds(pl.multiple_of(index % spec_dev * frame_len + cols, chunk), chunk)
            if len(volt_refs) == 2:
                here = own_at[0] == part
                return jnp.where(here, volt_refs[0][:, at], volt_refs[1][:, at]).astype(jnp.float32)
            return volt_refs[0][part, :, at].astype(jnp.float32)

        def body(turn, carry):
            cols = pl.multiple_of(turn * chunk, chunk)
            at = pl.ds(cols, chunk)
            pieces = [frame(index, cols) for index in range(spec_total)]
            taps = [taps_ref[tap : tap + 1, at] for tap in range(tap_count)]
            for spec in range(spec_total):
                total = None
                for tap in range(tap_count):
                    index = spec + tap - (tap_count - 1)
                    if index >= 0:
                        term = pieces[index] * taps[tap]
                        total = term if total is None else total + term
                frames[spec * rows : (spec + 1) * rows, at] = total.astype(jnp.bfloat16)
            return carry

        lax.fori_loop(0, frame_len // chunk, body, 0)

    if pieces_of_sum == 1:
        spectra = jnp.dot(frames[...], table_ref[...], preferred_element_type=jnp.float32)
    else:
        depth = frame_len // pieces_of_sum
        sums[...] = jnp.zeros_like(sums)

        def add(turn, carry):
            at = pl.ds(pl.multiple_of(turn * depth, depth), depth)
            sums[...] += jnp.dot(
                frames[:, at], table_ref[at, :], preferred_element_type=jnp.float32
            )
            return carry

        lax.fori_loop(0, pieces_of_sum, add, 0)
        spectra = sums[...]
    for group in range(table_ref.shape[1] // (2 * GROUP)):
        lanes = slice(group * 2 * GROUP, (group + 1) * 2 * GROUP)
        packed = jnp.concatenate(
            [spectra[s * rows : (s + 1) * rows, lanes] for s in range(spec_total)], axis=1
        )
        out_ref[:, group * width : (group + 1) * width] = packed.astype(jnp.bfloat16)


def block_spectra(own_at, volts, tap_weights, table, spec_total, pieces_of_sum=1):
    rows = volts[0].shape[-2]
    frame_len, cols = table.shape
    step = min(cols, 256 if pieces_of_sum == 1 else 128)
    width = cols * spec_total
    steps = cols // step

    def whole(array):
        return pl.BlockSpec(array.shape, lambda i, at: (0,) * array.ndim)

    return pl.pallas_call(
        functools.partial(spectra_kernel, pieces_of_sum),
        grid_spec=pltpu.PrefetchScalarGridSpec(
            num_scalar_prefetch=1,
            grid=(steps,),
            in_specs=[whole(v) for v in volts]
            + [whole(tap_weights), pl.BlockSpec((frame_len, step), lambda i, at: (0, i))],
            out_specs=pl.BlockSpec((rows, width // steps), lambda i, at: (0, i)),
            scratch_shapes=[
                pltpu.VMEM((spec_total * rows, frame_len), jnp.bfloat16),
                pltpu.VMEM((spec_total * rows, step), jnp.float32),
            ],
        ),
        out_shape=jax.ShapeDtypeStruct((rows, width), jnp.bfloat16),
        compiler_params=pltpu.CompilerParams(vmem_limit_bytes=VMEM_BYTES),
        cost_estimate=pl.CostEstimate(
            flops=2 * rows * spec_total * frame_len * cols,
            bytes_accessed=2 * (frame_len * cols + 2 * rows * width),
            transcendentals=0,
        ),
        name="spectra",
    )(own_at, *volts, tap_weights, table)


def vis_kernel(spec_total, jobs, unroll, base, chained, *refs):
    refs = list(refs)
    slots = None if base is None else refs.pop(0)
    own_ref, *their_refs = refs[: 1 + jobs]
    refs = refs[1 + jobs + chained :]
    out_ref, masks, buffers, sems = refs
    rows, lanes = own_ref.shape
    width = 2 * GROUP * spec_total
    groups = masks.shape[0]
    depth = buffers.shape[1]
    window = groups * width
    spans = []
    for group in range(groups):
        low = group * width // 128 * 128
        high = -(-(group + 1) * width // 128) * 128
        spans.append((low, high))
        lane = lax.broadcasted_iota(jnp.int32, (16, high - low), 1) + (low - group * width)
        inside = (lane >= 0) & (lane < width)
        chan, real = lane % GROUP, lane // GROUP % 2 == 0

        def put(index, where, value):
            masks[group, index] = jnp.where(inside & where, value, 0.0).astype(jnp.bfloat16)

        for c in range(HALF):
            put(c, chan % HALF == c, 1.0)
        for side, half in enumerate((chan < HALF, chan >= HALF)):
            put(HALF + 3 * side, half, 1.0)
            put(HALF + 3 * side + 1, half & real, -1.0)
            put(HALF + 3 * side + 2, half & ~real, 1.0)

    def copy_out(job, turn, slot):
        to = out_ref if slots is None else out_ref.at[slots[base + job]]
        count = groups * GROUP
        return pltpu.make_async_copy(
            buffers.at[job, slot], to.at[pl.ds(turn * count, count)], sems.at[job, slot]
        )

    turns = lanes // window
    unroll = math.gcd(unroll, turns)

    def body(step, carry):
        for ahead in range(unroll):
            turn = step * unroll + ahead
            for job in range(jobs):

                @pl.when(turn >= depth)
                def _():
                    copy_out(job, turn - depth, turn % depth).wait()

        for ahead in range(unroll):
            turn = step * unroll + ahead
            for group in range(groups):
                multiply(turn, group)
        for ahead in range(unroll):
            turn = step * unroll + ahead
            for job in range(jobs):
                copy_out(job, turn, turn % depth).start()
        return carry

    def multiply(turn, group):
        slot = turn % depth
        low, high = spans[group]
        span = high - low
        at = pl.ds(pl.multiple_of(turn * window + low, 128), span)

        def masked(block, index):
            tiles = block.reshape(rows // 16, 16, span) * masks[group, index][None]
            return tiles.reshape(rows, span)

        mine = own_ref[:, at]
        left = jnp.concatenate([masked(mine, c) for c in range(HALF)], axis=0)
        for job in range(jobs):
            theirs = their_refs[job][:, at]
            wide = theirs.astype(jnp.float32)
            ahead = pltpu.roll(wide, span - GROUP, 1).astype(jnp.bfloat16)
            behind = pltpu.roll(wide, GROUP, 1).astype(jnp.bfloat16)
            right = []
            for base in (HALF, HALF + 3):
                right.append(masked(theirs, base))
                right.append(masked(ahead, base + 1) + masked(behind, base + 2))
            product = lax.dot_general(
                left,
                jnp.concatenate(right, axis=0),
                (((1,), (1,)), ((), ())),
                preferred_element_type=jnp.float32,
            )
            product = (product * (1.0 / spec_total)).astype(jnp.bfloat16)
            for c in range(HALF):
                piece = product[c * rows : (c + 1) * rows]
                buffers[job, slot, group * GROUP + c] = piece[:, : 2 * rows]
                buffers[job, slot, group * GROUP + c + HALF] = piece[:, 2 * rows :]

    lax.fori_loop(0, turns // unroll, body, 0)
    for turn in range(max(turns - depth, 0), turns):
        for job in range(jobs):
            copy_out(job, turn, turn % depth).wait()


def visibility(own, theirs, spec_total, slots=None, base=None, into=None, unroll=1):
    rows, lanes = own.shape
    width = 2 * GROUP * spec_total
    chan_dev = lanes // (2 * spec_total)
    jobs = len(theirs)
    groups = min(math.lcm(width, 128) // width, chan_dev // GROUP)
    span = max(
        -(-(g + 1) * width // 128) * 128 - g * width // 128 * 128 for g in range(groups)
    )
    shape = (chan_dev, rows, 2 * rows)
    if slots is not None:
        shape = slots.shape + shape
    depth = max(4 if jobs == 1 else 2, 2 * unroll)
    in_vmem = pl.BlockSpec(memory_space=pltpu.VMEM)
    anywhere = pl.BlockSpec(memory_space=pltpu.HBM)
    args, specs, alias = [own, *theirs], [in_vmem] * (1 + jobs), {}
    if slots is not None:
        args.insert(0, slots)
        specs.insert(0, pl.BlockSpec(memory_space=pltpu.SMEM))
    if into is not None:
        alias = {len(args): 0}
        args.append(into)
        specs.append(anywhere)
    return pl.pallas_call(
        functools.partial(
            vis_kernel, spec_total, jobs, unroll, base, into is not None
        ),
        in_specs=specs,
        out_specs=anywhere,
        out_shape=pltpu.HBM(shape, jnp.bfloat16),
        scratch_shapes=[
            pltpu.VMEM((groups, HALF + 6, 16, span), jnp.bfloat16),
            pltpu.VMEM((jobs, depth, groups * GROUP, rows, 2 * rows), jnp.bfloat16),
            pltpu.SemaphoreType.DMA((jobs, depth)),
        ],
        input_output_aliases=alias,
        compiler_params=pltpu.CompilerParams(vmem_limit_bytes=VIS_BYTES),
        cost_estimate=pl.CostEstimate(
            flops=jobs * 4 * lanes * rows * rows * HALF,
            bytes_accessed=2 * (jobs + 1) * rows * lanes + 4 * jobs * chan_dev * rows * rows,
            transcendentals=0,
        ),
        name="vis",
    )(*args)


def order_kernel(block_total, offsets_ref, rounds_ref, sorted_ref):
    count = offsets_ref.shape[0]
    values = [offsets_ref[i] for i in range(count)]
    keys = [
        jnp.minimum(value, block_total - value) * count + i for i, value in enumerate(values)
    ]
    for i in range(count):
        place = sum(jnp.where(key < keys[i], 1, 0) for key in keys)
        rounds_ref[place] = i
        sorted_ref[place] = values[i] - 1


def order_rounds(pair_offsets, block_total):
    like = jax.ShapeDtypeStruct(pair_offsets.shape, jnp.int32)
    in_smem = pl.BlockSpec(memory_space=pltpu.SMEM)
    return pl.pallas_call(
        functools.partial(order_kernel, block_total),
        in_specs=[in_smem],
        out_specs=[in_smem, in_smem],
        out_shape=[like, like],
        name="order",
    )(pair_offsets)


def per_device(voltages, tap_weights, pair_offsets):
    rows, samples_dev = voltages.shape
    frame_len = tap_weights.shape[1]
    tm_count = lax.axis_size("tm")
    block_total = lax.axis_size("inp")
    chan_dev = frame_len // 2 // tm_count
    spec_total = samples_dev * tm_count // frame_len
    round_count = pair_offsets.shape[0]

    rounds, offsets = order_rounds(pair_offsets, block_total)
    own_at = lax.axis_index("tm").astype(jnp.int32).reshape(1)
    last = round_count - 1

    def exchange(place, beside=None):
        def branch(distance, block, *rest):
            theirs = from_ahead(block, distance)
            return (theirs,) if beside is None else (theirs, beside(block, *rest))

        def run(*args):
            branches = [functools.partial(branch, d) for d in range(1, block_total)]
            return lax.switch(offsets[place], branches, *args)

        return run

    def make_table(block, at):
        return dft_table(at, frame_len, chan_dev)

    def swapped(block):
        return [block, lax.ppermute(block, "tm", [(0, 1), (1, 0)])]

    def spectra_of(volts, table):
        return block_spectra(own_at, volts, tap_weights, table, spec_total)

    def spectra_part(own, at, taps, table, *volts):
        return block_spectra(at, volts, taps, table, spec_total, 4)

    def auto_part(own):
        return visibility(own, [own], spec_total)

    def cross_part(own, slots, *theirs):
        return visibility(own, theirs, spec_total, slots, 0)

    if tm_count == 2 and block_total <= 16:
        volts = swapped(voltages)
        if last:
            raw, table = exchange(last - 1, make_table)(voltages, own_at)
        else:
            table = make_table(voltages, own_at)
        own = spectra_of(volts, table)
        if last:
            raw = swapped(raw)
        theirs, hidden = [], None
        if last > 1:
            first, auto = exchange(0, auto_part)(own)
            theirs.append(first)
        else:
            auto = auto_part(own)
        for place in range(1, last - 1):
            if hidden is None:
                nearer, hidden = exchange(place, spectra_part)(
                    own, own_at, tap_weights, table, *raw
                )
            else:
                nearer = exchange(place)(own)[0]
            theirs.append(nearer)
        if last:
            theirs.append(spectra_of(raw, table) if hidden is None else hidden)
            final, cross = exchange(last, cross_part)(own, rounds, *theirs)
        else:
            final, cross = exchange(last)(own)[0], None
    else:
        table = make_table(voltages, own_at)
        own = spectra_of([lax.all_gather(voltages, "tm")], table)
        auto = auto_part(own)
        theirs = [exchange(place)(own)[0] for place in range(last)]
        final = exchange(last)(own)[0]
        cross = cross_part(own, rounds, *theirs) if last else None
    cross = visibility(own, [final], spec_total, rounds, last, cross, unroll=4)
    return cross, auto


def solution(mesh):
    in_specs = (P("inp", "tm"), P(), P())
    out_specs = (P(None, "tm", "inp", None), P("tm", "inp", None))
    return jax.shard_map(
        per_device, mesh=mesh, in_specs=in_specs, out_specs=out_specs, check_vma=False
    )
```

```python
import functools
import math

import jax
import jax.numpy as jnp
from jax import lax
from jax.experimental import pallas as pl
from jax.experimental.pallas import tpu as pltpu
from jax.sharding import PartitionSpec as P

GROUP = 16
HALF = GROUP // 2
VMEM_BYTES = 48 << 20
VIS_BYTES = 12 << 20


def from_ahead(block, distance):
    count = lax.axis_size("inp")
    return lax.ppermute(
        block, "inp", [(i, (i - distance) % count) for i in range(count)]
    )


def circle(steps, count):
    quarter = (steps + count // 8) // (count // 4)
    x = (steps - quarter * (count // 4)).astype(jnp.float32) * (2.0 * math.pi / count)
    square = x * x
    even = jnp.float32(-1.0 / math.factorial(10))
    odd = jnp.float32(1.0 / math.factorial(9))
    for power in (8, 6, 4, 2, 0):
        even = even * square + (-1.0) ** (power // 2) / math.factorial(power)
    for power in (7, 5, 3, 1):
        odd = odd * square + (-1.0) ** (power // 2) / math.factorial(power)
    odd = odd * x
    cross = quarter % 2 == 1
    cosine = jnp.where(cross, odd, even)
    sine = jnp.where(cross, even, odd)
    quarter = quarter % 4
    cosine = jnp.where((quarter == 1) | (quarter == 2), -cosine, cosine)
    sine = jnp.where(quarter >= 2, -sine, sine)
    return cosine, sine


def table_kernel(fine, chan_dev, own_at, out_ref, cos_a, sin_a, cos_b, sin_b):
    frame_len, lanes = out_ref.shape
    scale = 1.0 / math.sqrt(frame_len)
    shape = (8, lanes)
    column = lax.broadcasted_iota(jnp.int32, shape, 1) + pl.program_id(0) * lanes
    chan = own_at[0] * chan_dev + column // (2 * GROUP) * GROUP + column % GROUP
    quarter = column // GROUP % 2 * (frame_len // 4)
    row = lax.broadcasted_iota(jnp.int32, shape, 0)

    def coarse_rows(turn, carry):
        at = pl.ds(pl.multiple_of(turn * 8, 8), 8)
        cosine, sine = circle((row + turn * 8) * fine * chan % frame_len, frame_len)
        cos_a[at, :] = cosine * scale
        sin_a[at, :] = sine * scale
        return carry

    def fine_rows(turn, carry):
        at = pl.ds(pl.multiple_of(turn * 8, 8), 8)
        steps = ((row + turn * 8) * chan + quarter) % frame_len
        cos_b[at, :], sin_b[at, :] = circle(steps, frame_len)
        return carry

    def body(turn, carry):
        at = pl.ds(turn, 1)
        block = cos_a[at, :] * cos_b[...] - sin_a[at, :] * sin_b[...]
        out_ref[pl.ds(pl.multiple_of(turn * fine, fine), fine), :] = block.astype(jnp.bfloat16)
        return carry

    lax.fori_loop(0, frame_len // fine // 8, coarse_rows, 0)
    lax.fori_loop(0, fine // 8, fine_rows, 0)
    lax.fori_loop(0, frame_len // fine, body, 0)


def dft_table(own_at, frame_len, chan_dev):
    fine, lanes = 64, 128
    parts = [pltpu.VMEM((frame_len // fine, lanes), jnp.float32)] * 2
    parts += [pltpu.VMEM((fine, lanes), jnp.float32)] * 2
    return pl.pallas_call(
        functools.partial(table_kernel, fine, chan_dev),
        grid=(2 * chan_dev // lanes,),
        in_specs=[pl.BlockSpec(memory_space=pltpu.SMEM)],
        out_specs=pl.BlockSpec((frame_len, lanes), lambda i: (0, i)),
        out_shape=pltpu.HBM((frame_len, 2 * chan_dev), jnp.bfloat16),
        scratch_shapes=parts,
        compiler_params=pltpu.CompilerParams(vmem_limit_bytes=VIS_BYTES),
        cost_estimate=pl.CostEstimate(
            flops=6 * frame_len * chan_dev,
            bytes_accessed=4 * frame_len * chan_dev,
            transcendentals=0,
        ),
        name="table",
    )(own_at)


def spectra_kernel(pieces_of_sum, own_at, *refs):
    *volt_refs, taps_ref, table_ref, out_ref, frames, sums = refs
    rows, samples_dev = volt_refs[0].shape[-2:]
    tap_count, frame_len = taps_ref.shape
    spec_dev = samples_dev // frame_len
    spec_total = frames.shape[0] // rows
    width = 2 * GROUP * spec_total

    @pl.when(pl.program_id(0) == 0)
    def _():
        chunk = 256

        def frame(index, cols):
            part = index // spec_dev
            at = pl.ds(pl.multiple_of(index % spec_dev * frame_len + cols, chunk), chunk)
            if len(volt_refs) == 2:
                here = own_at[0] == part
                return jnp.where(here, volt_refs[0][:, at], volt_refs[1][:, at]).astype(jnp.float32)
            return volt_refs[0][part, :, at].astype(jnp.float32)

        def body(turn, carry):
            cols = pl.multiple_of(turn * chunk, chunk)
            at = pl.ds(cols, chunk)
            pieces = [frame(index, cols) for index in range(spec_total)]
            taps = [taps_ref[tap : tap + 1, at] for tap in range(tap_count)]
            for spec in range(spec_total):
                total = None
                for tap in range(tap_count):
                    index = spec + tap - (tap_count - 1)
                    if index >= 0:
                        term = pieces[index] * taps[tap]
                        total = term if total is None else total + term
                frames[spec * rows : (spec + 1) * rows, at] = total.astype(jnp.bfloat16)
            return carry

        lax.fori_loop(0, frame_len // chunk, body, 0)

    if pieces_of_sum == 1:
        spectra = jnp.dot(frames[...], table_ref[...], preferred_element_type=jnp.float32)
    else:
        depth = frame_len // pieces_of_sum
        sums[...] = jnp.zeros_like(sums)

        def add(turn, carry):
            at = pl.ds(pl.multiple_of(turn * depth, depth), depth)
            sums[...] += jnp.dot(
                frames[:, at], table_ref[at, :], preferred_element_type=jnp.float32
            )
            return carry

        lax.fori_loop(0, pieces_of_sum, add, 0)
        spectra = sums[...]
    for group in range(table_ref.shape[1] // (2 * GROUP)):
        lanes = slice(group * 2 * GROUP, (group + 1) * 2 * GROUP)
        packed = jnp.concatenate(
            [spectra[s * rows : (s + 1) * rows, lanes] for s in range(spec_total)], axis=1
        )
        out_ref[:, group * width : (group + 1) * width] = packed.astype(jnp.bfloat16)


def block_spectra(own_at, volts, tap_weights, table, spec_total, pieces_of_sum=1):
    rows = volts[0].shape[-2]
    frame_len, cols = table.shape
    step = min(cols, 256)
    width = cols * spec_total
    steps = cols // step

    def whole(array):
        return pl.BlockSpec(array.shape, lambda i, at: (0,) * array.ndim)

    return pl.pallas_call(
        functools.partial(spectra_kernel, pieces_of_sum),
        grid_spec=pltpu.PrefetchScalarGridSpec(
            num_scalar_prefetch=1,
            grid=(steps,),
            in_specs=[whole(v) for v in volts]
            + [whole(tap_weights), pl.BlockSpec((frame_len, step), lambda i, at: (0, i))],
            out_specs=pl.BlockSpec((rows, width // steps), lambda i, at: (0, i)),
            scratch_shapes=[
                pltpu.VMEM((spec_total * rows, frame_len), jnp.bfloat16),
                pltpu.VMEM((spec_total * rows, step), jnp.float32),
            ],
        ),
        out_shape=jax.ShapeDtypeStruct((rows, width), jnp.bfloat16),
        compiler_params=pltpu.CompilerParams(vmem_limit_bytes=VMEM_BYTES),
        cost_estimate=pl.CostEstimate(
            flops=2 * rows * spec_total * frame_len * cols,
            bytes_accessed=2 * (frame_len * cols + 2 * rows * width),
            transcendentals=0,
        ),
        name="spectra",
    )(own_at, *volts, tap_weights, table)


def vis_kernel(spec_total, jobs, unroll, base, chained, *refs):
    refs = list(refs)
    slots = None if base is None else refs.pop(0)
    own_ref, *their_refs = refs[: 1 + jobs]
    refs = refs[1 + jobs + chained :]
    out_ref, masks, buffers, sems = refs
    rows, lanes = own_ref.shape
    width = 2 * GROUP * spec_total
    groups = masks.shape[0]
    depth = buffers.shape[1]
    window = groups * width
    spans = []
    for group in range(groups):
        low = group * width // 128 * 128
        high = -(-(group + 1) * width // 128) * 128
        spans.append((low, high))
        lane = lax.broadcasted_iota(jnp.int32, (16, high - low), 1) + (low - group * width)
        inside = (lane >= 0) & (lane < width)
        chan, real = lane % GROUP, lane // GROUP % 2 == 0

        def put(index, where, value):
            masks[group, index] = jnp.where(inside & where, value, 0.0).astype(jnp.bfloat16)

        for c in range(HALF):
            put(c, chan % HALF == c, 1.0)
        for side, half in enumerate((chan < HALF, chan >= HALF)):
            put(HALF + 3 * side, half, 1.0)
            put(HALF + 3 * side + 1, half & real, -1.0)
            put(HALF + 3 * side + 2, half & ~real, 1.0)

    def copy_out(job, turn, slot):
        to = out_ref if slots is None else out_ref.at[slots[base + job]]
        count = groups * GROUP
        return pltpu.make_async_copy(
            buffers.at[job, slot], to.at[pl.ds(turn * count, count)], sems.at[job, slot]
        )

    turns = lanes // window
    unroll = math.gcd(unroll, turns)

    def body(step, carry):
        for ahead in range(unroll):
            turn = step * unroll + ahead
            for job in range(jobs):

                @pl.when(turn >= depth)
                def _():
                    copy_out(job, turn - depth, turn % depth).wait()

        for ahead in range(unroll):
            turn = step * unroll + ahead
            for group in range(groups):
                multiply(turn, group)
        for ahead in range(unroll):
            turn = step * unroll + ahead
            for job in range(jobs):
                copy_out(job, turn, turn % depth).start()
        return carry

    def multiply(turn, group):
        slot = turn % depth
        low, high = spans[group]
        span = high - low
        at = pl.ds(pl.multiple_of(turn * window + low, 128), span)

        def masked(block, index):
            tiles = block.reshape(rows // 16, 16, span) * masks[group, index][None]
            return tiles.reshape(rows, span)

        mine = own_ref[:, at]
        left = jnp.concatenate([masked(mine, c) for c in range(HALF)], axis=0)
        for job in range(jobs):
            theirs = their_refs[job][:, at]
            wide = theirs.astype(jnp.float32)
            ahead = pltpu.roll(wide, span - GROUP, 1).astype(jnp.bfloat16)
            behind = pltpu.roll(wide, GROUP, 1).astype(jnp.bfloat16)
            right = []
            for base in (HALF, HALF + 3):
                right.append(masked(theirs, base))
                right.append(masked(ahead, base + 1) + masked(behind, base + 2))
            product = lax.dot_general(
                left,
                jnp.concatenate(right, axis=0),
                (((1,), (1,)), ((), ())),
                preferred_element_type=jnp.float32,
            )
            product = (product * (1.0 / spec_total)).astype(jnp.bfloat16)
            for c in range(HALF):
                piece = product[c * rows : (c + 1) * rows]
                buffers[job, slot, group * GROUP + c] = piece[:, : 2 * rows]
                buffers[job, slot, group * GROUP + c + HALF] = piece[:, 2 * rows :]

    lax.fori_loop(0, turns // unroll, body, 0)
    for turn in range(max(turns - depth, 0), turns):
        for job in range(jobs):
            copy_out(job, turn, turn % depth).wait()


def visibility(own, theirs, spec_total, slots=None, base=None, into=None, unroll=1):
    rows, lanes = own.shape
    width = 2 * GROUP * spec_total
    chan_dev = lanes // (2 * spec_total)
    jobs = len(theirs)
    groups = min(math.lcm(width, 128) // width, chan_dev // GROUP)
    span = max(
        -(-(g + 1) * width // 128) * 128 - g * width // 128 * 128 for g in range(groups)
    )
    shape = (chan_dev, rows, 2 * rows)
    if slots is not None:
        shape = slots.shape + shape
    depth = max(4 if jobs == 1 else 2, 2 * unroll)
    in_vmem = pl.BlockSpec(memory_space=pltpu.VMEM)
    anywhere = pl.BlockSpec(memory_space=pltpu.HBM)
    args, specs, alias = [own, *theirs], [in_vmem] * (1 + jobs), {}
    if slots is not None:
        args.insert(0, slots)
        specs.insert(0, pl.BlockSpec(memory_space=pltpu.SMEM))
    if into is not None:
        alias = {len(args): 0}
        args.append(into)
        specs.append(anywhere)
    return pl.pallas_call(
        functools.partial(
            vis_kernel, spec_total, jobs, unroll, base, into is not None
        ),
        in_specs=specs,
        out_specs=anywhere,
        out_shape=pltpu.HBM(shape, jnp.bfloat16),
        scratch_shapes=[
            pltpu.VMEM((groups, HALF + 6, 16, span), jnp.bfloat16),
            pltpu.VMEM((jobs, depth, groups * GROUP, rows, 2 * rows), jnp.bfloat16),
            pltpu.SemaphoreType.DMA((jobs, depth)),
        ],
        input_output_aliases=alias,
        compiler_params=pltpu.CompilerParams(vmem_limit_bytes=VIS_BYTES),
        cost_estimate=pl.CostEstimate(
            flops=jobs * 4 * lanes * rows * rows * HALF,
            bytes_accessed=2 * (jobs + 1) * rows * lanes + 4 * jobs * chan_dev * rows * rows,
            transcendentals=0,
        ),
        name="vis",
    )(*args)


def order_kernel(block_total, offsets_ref, rounds_ref, sorted_ref):
    count = offsets_ref.shape[0]
    values = [offsets_ref[i] for i in range(count)]
    keys = [
        jnp.minimum(value, block_total - value) * count + i for i, value in enumerate(values)
    ]
    for i in range(count):
        place = sum(jnp.where(key < keys[i], 1, 0) for key in keys)
        rounds_ref[place] = i
        sorted_ref[place] = values[i] - 1


def order_rounds(pair_offsets, block_total):
    like = jax.ShapeDtypeStruct(pair_offsets.shape, jnp.int32)
    in_smem = pl.BlockSpec(memory_space=pltpu.SMEM)
    return pl.pallas_call(
        functools.partial(order_kernel, block_total),
        in_specs=[in_smem],
        out_specs=[in_smem, in_smem],
        out_shape=[like, like],
        name="order",
    )(pair_offsets)


def per_device(voltages, tap_weights, pair_offsets):
    rows, samples_dev = voltages.shape
    frame_len = tap_weights.shape[1]
    tm_count = lax.axis_size("tm")
    block_total = lax.axis_size("inp")
    chan_dev = frame_len // 2 // tm_count
    spec_total = samples_dev * tm_count // frame_len
    round_count = pair_offsets.shape[0]

    rounds, offsets = order_rounds(pair_offsets, block_total)
    own_at = lax.axis_index("tm").astype(jnp.int32).reshape(1)
    last = round_count - 1

    def exchange(place, beside=None):
        def branch(distance, block, *rest):
            theirs = from_ahead(block, distance)
            return (theirs,) if beside is None else (theirs, beside(block, *rest))

        def run(*args):
            branches = [functools.partial(branch, d) for d in range(1, block_total)]
            return lax.switch(offsets[place], branches, *args)

        return run

    def make_table(block, at):
        return dft_table(at, frame_len, chan_dev)

    def swapped(block):
        return [block, lax.ppermute(block, "tm", [(0, 1), (1, 0)])]

    def spectra_of(volts, table):
        return block_spectra(own_at, volts, tap_weights, table, spec_total)

    def spectra_part(own, at, taps, table, *volts):
        return block_spectra(at, volts, taps, table, spec_total, 8)

    def auto_part(own):
        return visibility(own, [own], spec_total)

    def cross_part(own, slots, *theirs):
        return visibility(own, theirs, spec_total, slots, 0)

    if tm_count == 2 and block_total <= 16:
        volts = swapped(voltages)
        if last:
            raw, table = exchange(last - 1, make_table)(voltages, own_at)
        else:
            table = make_table(voltages, own_at)
        own = spectra_of(volts, table)
        if last:
            raw = swapped(raw)
        theirs, hidden = [], None
        if last > 1:
            first, auto = exchange(0, auto_part)(own)
            theirs.append(first)
        else:
            auto = auto_part(own)
        for place in range(1, last - 1):
            if hidden is None:
                nearer, hidden = exchange(place, spectra_part)(
                    own, own_at, tap_weights, table, *raw
                )
            else:
                nearer = exchange(place)(own)[0]
            theirs.append(nearer)
        if last:
            theirs.append(spectra_of(raw, table) if hidden is None else hidden)
            final, cross = exchange(last, cross_part)(own, rounds, *theirs)
        else:
            final, cross = exchange(last)(own)[0], None
    else:
        table = make_table(voltages, own_at)
        own = spectra_of([lax.all_gather(voltages, "tm")], table)
        auto = auto_part(own)
        theirs = [exchange(place)(own)[0] for place in range(last)]
        final = exchange(last)(own)[0]
        cross = cross_part(own, rounds, *theirs) if last else None
    cross = visibility(own, [final], spec_total, rounds, last, cross, unroll=4)
    return cross, auto


def solution(mesh):
    in_specs = (P("inp", "tm"), P(), P())
    out_specs = (P(None, "tm", "inp", None), P("tm", "inp", None))
    return jax.shard_map(
        per_device, mesh=mesh, in_specs=in_specs, out_specs=out_specs, check_vma=False
    )
```
